32 devices in a mesh: problem: 2 (over y), worker: 4 (over z), head: 4 (over x, core).
Axes of the slice: x: 2, y: 2, z: 4, core: 2. Of those that a mesh axis runs over, the one named last changes fastest.
Arguments:
- queries: bfloat16 [8, 4, 40, 128], P(('problem', 'worker'), None, 'head'), parts along dimension 0, may hold values from -60 to 60
- cache_keys: bfloat16 [8, 2048, 8, 128], P(('problem', 'worker'), None, 'head'), parts along dimension 0, may hold values from -6 to 6
- cache_values: bfloat16 [8, 2048, 8, 128], P(('problem', 'worker'), None, 'head'), parts along dimension 0, may hold values from -6 to 6
- new_keys: bfloat16 [8, 4, 8, 128], P(('problem', 'worker'), None, 'head'), parts along dimension 0, may hold values from -6 to 6
- new_values: bfloat16 [8, 4, 8, 128], P(('problem', 'worker'), None, 'head'), parts along dimension 0, may hold values from -6 to 6
- lengths: int32 [8, 4], P(('problem', 'worker')), parts along dimension 0, may hold values from 1 to 2048, as said below
Outputs:
- attended: bfloat16 [8, 4, 40, 128], P(('problem', 'worker'), None, 'head'), parts along dimension 0
The draws below stay inside these ranges and needn't reach their ends.
There are 2 independent parts, one for each index of `problem`. The reference program is written for one: setup_inputs(seed, part) draws one part's arguments, and reference() takes and returns one part's arrays. A program takes and returns all parts, laid end to end along the dimension named above; each array names one. Nothing has to cross between parts.
Inputs may be any that keep to these rules, and one draw needn't show every extreme that they name: lengths never fall from one step to the next; some worker's length at the last step is exactly 2048.
All inputs are finite; a program needn't handle non-finite values.
Results may differ from the reference program's by a relative error of at most 0.005.
Values may be sent and summed in bfloat16 or wider, within the bound.
A program may use at most 64 MiB of HBM per device.

```python
import jax
import jax.numpy as jnp
from jax import lax

Q_HEADS = 40
KV_HEADS = 8
HEAD_DIM = 128
GROUP_SIZE = 5
CACHE_LEN = 2048
DECODE_STEPS = 4
WORKERS = 4


def draw_queries(key, part):
    full_shape = (WORKERS, DECODE_STEPS, Q_HEADS, HEAD_DIM)
    result = jnp.clip(3.0 * jax.random.normal(jax.random.fold_in(key, 1), full_shape, jnp.float32), -18.0, 18.0)
    return result.astype(jnp.bfloat16)


def draw_cache_keys(key, part):
    full_shape = (WORKERS, CACHE_LEN, KV_HEADS, HEAD_DIM)
    result = jnp.clip(jax.random.normal(jax.random.fold_in(key, 2), full_shape, jnp.float32), -6.0, 6.0)
    return result.astype(jnp.bfloat16)


def draw_lengths(key, part):
    base_key = jax.random.fold_in(key, 3)
    shift_key, trim_key, growth_key, longest_key = jax.random.split(base_key, 4)
    halving_count = jax.random.randint(shift_key, (WORKERS,), 0, 4, jnp.int32)
    upper_bound = jnp.right_shift(jnp.full((WORKERS,), CACHE_LEN, jnp.int32), halving_count)
    trimmed = jax.random.randint(trim_key, (WORKERS,), 0, CACHE_LEN // 16 + 1, jnp.int32)
    starting = upper_bound - trimmed
    longest = jax.random.randint(longest_key, (), 0, WORKERS, jnp.int32)
    worker_ids = jnp.arange(WORKERS, dtype=jnp.int32)
    starting = jnp.where(worker_ids == longest, CACHE_LEN, starting)
    growth = jax.random.randint(growth_key, (WORKERS,), 0, 4, jnp.int32)
    step_ids = jnp.arange(DECODE_STEPS, dtype=jnp.int32)
    result = starting[:, None] - (DECODE_STEPS - 1 - step_ids)[None, :] * growth[:, None]
    return jnp.maximum(result, 1).astype(jnp.int32)


def steps_of(rng, extent, cuts, least, largest):
    factor_of, own = 1.0, jax.random.fold_in(rng, 6)
    for dim, shards_of in cuts:
        heights = jnp.exp(jax.random.uniform(jax.random.fold_in(own, dim), (shards_of,), jnp.float32, least / len(cuts), largest / len(cuts)))
        factor_of = factor_of * jnp.repeat(heights, extent[dim] // shards_of).reshape([-1 if axis == dim else 1 for axis in range(len(extent))])
    return factor_of


def bell_draw(own_key, dims, scale, limit, cuts=(), held_as=jnp.bfloat16):
    values = scale * jax.random.normal(own_key, dims, jnp.float32)
    if cuts:
        values = values * steps_of(own_key, dims, cuts, -0.22, 0.18)
    return jnp.clip(values, -limit, limit).astype(held_as)


def setup_inputs(seed: int = 0, part: int = 0) -> dict:
    keys = jax.random.split(jax.random.key(seed), 7)
    own_keys = jax.random.split(jax.random.fold_in(keys[6], part), 7)
    queries = draw_queries(jax.random.fold_in(jax.random.fold_in(keys[6], part), 71), part)
    cache_keys = draw_cache_keys(jax.random.fold_in(jax.random.fold_in(keys[6], part), 71), part)
    cache_values = bell_draw(own_keys[2], (WORKERS, CACHE_LEN, KV_HEADS, HEAD_DIM), 1.0, 6.0, ((0, 4), (2, 4)))
    new_keys = bell_draw(own_keys[3], (WORKERS, DECODE_STEPS, KV_HEADS, HEAD_DIM), 1.0, 6.0, ((0, 4), (2, 4)))
    new_values = bell_draw(own_keys[4], (WORKERS, DECODE_STEPS, KV_HEADS, HEAD_DIM), 1.0, 6.0, ((0, 4), (2, 4)))
    lengths = draw_lengths(jax.random.fold_in(jax.random.fold_in(keys[6], part), 71), part)
    return dict(queries=queries, cache_keys=cache_keys, cache_values=cache_values, new_keys=new_keys, new_values=new_values, lengths=lengths)


masked_score = -1.0e30


def fold_block(running, scores, visible, value_rows):
    maxima, totals, outputs = running
    fresh_max = jnp.maximum(maxima, jnp.max(jnp.where(visible, scores, masked_score), axis=-1))
    carried = jnp.exp(maxima - fresh_max)
    weights = jnp.where(visible, jnp.exp(scores - fresh_max[..., None]), 0.0)
    totals = totals * carried + jnp.sum(weights, axis=-1)
    rounded = weights.astype(jnp.bfloat16).astype(jnp.float32)
    outputs = outputs * carried[..., None] + jnp.einsum("krc,ckd->krd", rounded, value_rows.astype(jnp.float32))
    return fresh_max, totals, outputs


def reference(queries, cache_keys, cache_values, new_keys, new_values, lengths):
    score_scale = 1.0 / (HEAD_DIM ** 0.5)
    row_count = WORKERS * DECODE_STEPS * GROUP_SIZE
    query_rows = queries.astype(jnp.float32).reshape(WORKERS, DECODE_STEPS, KV_HEADS, GROUP_SIZE, HEAD_DIM)
    query_rows = query_rows.transpose(2, 0, 1, 3, 4).reshape(KV_HEADS, row_count, HEAD_DIM)
    row_index = jnp.arange(row_count, dtype=jnp.int32)
    row_worker = row_index // (DECODE_STEPS * GROUP_SIZE)
    row_step = (row_index // GROUP_SIZE) % DECODE_STEPS
    fresh_keys = new_keys.reshape(WORKERS * DECODE_STEPS, KV_HEADS, HEAD_DIM)
    fresh_values = new_values.reshape(WORKERS * DECODE_STEPS, KV_HEADS, HEAD_DIM)
    column_index = jnp.arange(WORKERS * DECODE_STEPS, dtype=jnp.int32)
    column_worker = column_index // DECODE_STEPS
    column_step = column_index % DECODE_STEPS
    visible = (column_step[None, :] < row_step[:, None]) | ((column_step[None, :] == row_step[:, None]) & (column_worker[None, :] == row_worker[:, None]))
    running = (jnp.full((KV_HEADS, row_count), masked_score, jnp.float32), jnp.zeros((KV_HEADS, row_count), jnp.float32), jnp.zeros((KV_HEADS, row_count, HEAD_DIM), jnp.float32))
    scores = jnp.einsum("krd,ckd->krc", query_rows, fresh_keys.astype(jnp.float32)) * score_scale
    running = fold_block(running, scores, visible[None], fresh_values)
    slot_index = jnp.arange(CACHE_LEN, dtype=jnp.int32)

    def absorb(running, worker_item):
        worker_keys, worker_values, worker_lengths = worker_item
        visible_len = worker_lengths[row_step]
        cache_visible = slot_index[None, :] < visible_len[:, None]
        cache_scores = jnp.einsum("krd,ckd->krc", query_rows, worker_keys.astype(jnp.float32)) * score_scale
        return fold_block(running, cache_scores, cache_visible[None], worker_values), None

    running, _ = lax.scan(absorb, running, (cache_keys, cache_values, lengths))
    maxima, totals, outputs = running
    combined = outputs / totals[..., None]
    combined = combined.reshape(KV_HEADS, WORKERS, DECODE_STEPS, GROUP_SIZE, HEAD_DIM).transpose(1, 2, 0, 3, 4)
    return combined.reshape(WORKERS, DECODE_STEPS, Q_HEADS, HEAD_DIM).astype(jnp.bfloat16)
```

```python
import functools
import math

import jax
import jax.numpy as jnp
from jax import lax
from jax.experimental import pallas as pl
from jax.experimental.pallas import tpu as pltpu
from jax.sharding import PartitionSpec as P

masked_score = -1e30
lanes = 128
score_chunk = 512
value_chunk = 512
partial_type = jnp.bfloat16


def round_up(number, unit):
    return (number + unit - 1) // unit * unit


def partners_by_distance(own, workers):
    if workers > 8:
        return [lax.rem(own + step, workers) for step in range(1, workers)]
    table = [
        sorted((w for w in range(workers) if w != i), key=lambda w: (abs(w - i), w))
        for i in range(workers)
    ]
    partners = []
    for place in range(workers - 1):
        partner = jnp.int32(table[0][place])
        for i in range(1, workers):
            partner = jnp.where(own == i, table[i][place], partner)
        partners.append(partner)
    return partners


def kernel(
    workers,
    kv,
    steps,
    q_ref,
    k_ref,
    v_ref,
    nk_ref,
    nv_ref,
    len_ref,
    out_ref,
    q_in,
    q_pad,
    q_own,
    q_got,
    keys,
    values,
    new_keys,
    new_values,
    lens,
    score_buf,
    part_send,
    part_got,
    stat_send,
    stat_got,
    load_sem,
    q_send_sem,
    q_recv_sem,
    part_send_sem,
    part_recv_sem,
    stat_send_sem,
    stat_recv_sem,
):
    own = lax.axis_index("worker")
    rows_all, head_width = q_ref.shape
    per = rows_all // kv
    padded = q_pad.shape[0] // kv
    columns = k_ref.shape[0]
    fresh_columns = nk_ref.shape[0]
    factor = head_width ** (-0.5) * math.log2(math.e)
    partners = partners_by_distance(own, workers)

    barrier = pltpu.get_barrier_semaphore()
    for partner in partners:
        pl.semaphore_signal(
            barrier, inc=1, device_id={"worker": partner}, device_id_type=pl.DeviceIdType.MESH
        )

    loads = []
    for place, (source, target) in enumerate(
        (
            (q_ref, q_in),
            (len_ref, lens),
            (nk_ref, new_keys),
            (nv_ref, new_values),
            (k_ref, keys),
            (v_ref, values),
        )
    ):
        loads.append(pltpu.make_async_copy(source, target, load_sem.at[place]))
        loads[-1].start()

    loads[0].wait()
    q_pad[...] = jnp.zeros_like(q_pad)
    q_rows = q_in[...].astype(jnp.float32)
    for head in range(kv):
        q_pad[head * padded : head * padded + per, :] = q_rows[head * per : (head + 1) * per]
    q_own[...] = q_pad[...].astype(jnp.bfloat16)

    pl.semaphore_wait(barrier, workers - 1)
    sends = []

    def send(source, target, send_sem, recv_sem, partner):
        copy = pltpu.make_async_remote_copy(
            src_ref=source,
            dst_ref=target,
            send_sem=send_sem,
            recv_sem=recv_sem,
            device_id={"worker": partner},
            device_id_type=pl.DeviceIdType.MESH,
        )
        copy.start()
        sends.append(copy)

    for place, partner in reversed(list(enumerate(partners))):
        send(q_own, q_got.at[own], q_send_sem.at[place], q_recv_sem.at[own], partner)

    row_id = lax.broadcasted_iota(jnp.int32, (padded, lanes), 0)
    lane_id = lax.broadcasted_iota(jnp.int32, (padded, lanes), 1)
    row_step = lax.rem(row_id, steps)
    lane_head = lax.rem(lane_id, kv)
    loads[1].wait()
    limit = jnp.zeros((padded, lanes), jnp.int32)
    for step in range(steps):
        limit = jnp.where(row_step == step, lens[0, step], limit)
    limit = limit * kv - lane_id

    def fresh_limit(is_own):
        return jnp.minimum((row_step + (1 if is_own else 0)) * kv, fresh_columns) - lane_id

    loads[2].wait()
    loads[3].wait()
    tail = jnp.zeros((lanes - fresh_columns, head_width), jnp.float32)
    fresh_k = jnp.concatenate([new_keys[...].astype(jnp.float32), tail], axis=0)
    fresh_v = jnp.concatenate([new_values[...].astype(jnp.float32), tail], axis=0)
    fresh_k = fresh_k.astype(jnp.bfloat16)
    fresh_v = fresh_v.astype(jnp.bfloat16)

    full_row = lax.broadcasted_iota(jnp.int32, (kv * padded, lanes), 0)
    full_lane = lax.broadcasted_iota(jnp.int32, (kv * padded, lanes), 1)
    diagonal = full_row == full_lane

    def to_row(column):
        return jnp.sum(jnp.where(diagonal, column, 0.0), axis=0, keepdims=True)

    def to_column(row):
        return jnp.sum(jnp.where(diagonal, row, 0.0), axis=1, keepdims=True)

    def attend(queries, count, is_own, value_ready):
        best = [jnp.full((padded, lanes), masked_score, jnp.float32) for _ in range(count)]
        blocks = [
            (start, min(score_chunk, columns - start)) for start in range(0, columns, score_chunk)
        ] + [(columns, lanes)]
        for start, size in blocks:
            block = fresh_k if start == columns else keys[start : start + size, :]
            scores = lax.dot_general(
                queries, block, (((1,), (1,)), ((), ())), preferred_element_type=jnp.float32
            )
            for item in range(count):
                base = item * kv * padded
                for offset in range(0, size, lanes):
                    score = scores[base : base + padded, offset : offset + lanes]
                    for head in range(1, kv):
                        low = base + head * padded
                        score = jnp.where(
                            lane_head == head,
                            scores[low : low + padded, offset : offset + lanes],
                            score,
                        )
                    if start == columns:
                        seen = fresh_limit(is_own) > 0
                    else:
                        seen = limit > start + offset
                    score = jnp.where(seen, score, masked_score)
                    best[item] = jnp.maximum(best[item], score)
                    score_buf[
                        item * padded : (item + 1) * padded,
                        start + offset : start + offset + lanes,
                    ] = score
        maxima, pivots = [], []
        for item in range(count):
            heads = [
                jnp.max(
                    jnp.where(lane_head == head, best[item], masked_score), axis=1, keepdims=True
                )
                for head in range(kv)
            ]
            pivot = jnp.broadcast_to(heads[0], (padded, lanes))
            for head in range(1, kv):
                pivot = jnp.where(lane_head == head, heads[head], pivot)
            maxima.append(to_row(jnp.concatenate(heads, axis=0)))
            pivots.append(pivot)
        sums = [jnp.zeros((padded, lanes), jnp.float32) for _ in range(count)]
        outputs = jnp.zeros((count * kv * padded, head_width), jnp.float32)
        value_ready()
        blocks = [
            (start, min(value_chunk, columns - start)) for start in range(0, columns, value_chunk)
        ] + [(columns, lanes)]
        for start, size in blocks:
            pieces = []
            for offset in range(0, size, lanes):
                stack = []
                for item in range(count):
                    score = score_buf[
                        item * padded : (item + 1) * padded,
                        start + offset : start + offset + lanes,
                    ]
                    weight = jnp.exp2((score - pivots[item]) * factor)
                    sums[item] = sums[item] + weight
                    for head in range(kv):
                        stack.append(jnp.where(lane_head == head, weight, 0.0))
                pieces.append(jnp.concatenate(stack, axis=0).astype(jnp.bfloat16))
            weights = pieces[0] if len(pieces) == 1 else jnp.concatenate(pieces, axis=1)
            block = fresh_v if start == columns else values[start : start + size, :]
            outputs = outputs + jnp.dot(weights, block, preferred_element_type=jnp.float32)
        totals = []
        for item in range(count):
            heads = [
                jnp.sum(jnp.where(lane_head == head, sums[item], 0.0), axis=1, keepdims=True)
                for head in range(kv)
            ]
            totals.append(to_row(jnp.concatenate(heads, axis=0)))
        return maxima, totals, outputs

    loads[4].wait()
    own_max, own_total, own_out = attend(q_own[...], 1, True, loads[5].wait)
    own_max, own_total = own_max[0], own_total[0]

    def answer(place, partner):
        slot = q_got.at[partner]
        pltpu.make_async_copy(slot, slot, q_recv_sem.at[partner]).wait()
        maxima, totals, outputs = attend(q_got[partner], 1, False, lambda: None)
        stat_send[place, 0:1, :] = maxima[0]
        stat_send[place, 1:2, :] = totals[0]
        part_send[place] = outputs.astype(part_send.dtype)
        stat = pltpu.make_async_remote_copy(
            src_ref=stat_send.at[place],
            dst_ref=stat_got.at[own],
            send_sem=stat_send_sem.at[place],
            recv_sem=stat_recv_sem.at[own],
            device_id={"worker": partner},
            device_id_type=pl.DeviceIdType.MESH,
        )
        part = pltpu.make_async_remote_copy(
            src_ref=part_send.at[place],
            dst_ref=part_got.at[own],
            send_sem=part_send_sem.at[place],
            recv_sem=part_recv_sem.at[own],
            device_id={"worker": partner},
            device_id_type=pl.DeviceIdType.MESH,
        )
        stat.start()
        part.start()
        return stat, part

    if workers <= 8:
        for place, partner in enumerate(partners):
            sends.extend(answer(place, partner))
    else:

        def body(place, carry):
            answer(place, lax.rem(own + 1 + place, workers))
            return carry

        lax.fori_loop(0, workers - 1, body, 0)
        for place, partner in enumerate(partners):
            for source, sem in ((stat_send, stat_send_sem), (part_send, part_send_sem)):
                slot = source.at[place]
                pltpu.make_async_copy(slot, slot, sem.at[place]).wait()

    top = own_max
    for partner in partners:
        slot = stat_got.at[partner]
        pltpu.make_async_copy(slot, slot, stat_recv_sem.at[partner]).wait()
        top = jnp.maximum(top, stat_got[partner, 0:1, :])
    own_scale = jnp.exp2((own_max - top) * factor)
    total = own_total * own_scale
    scales = []
    for partner in partners:
        scale = jnp.exp2((stat_got[partner, 0:1, :] - top) * factor)
        total = total + stat_got[partner, 1:2, :] * scale
        scales.append(scale)
    merged = own_out * to_column(own_scale / total)
    columns_of = [to_column(scale / total) for scale in scales]
    for partner, column in zip(partners, columns_of):
        slot = part_got.at[partner]
        pltpu.make_async_copy(slot, slot, part_recv_sem.at[partner]).wait()
        merged = merged + part_got[partner].astype(jnp.float32) * column
    out_ref[...] = jnp.concatenate(
        [merged[head * padded : head * padded + per] for head in range(kv)], axis=0
    ).astype(out_ref.dtype)
    for copy in sends:
        copy.wait_send()


def local(queries, cache_keys, cache_values, new_keys, new_values, lengths):
    workers = lax.axis_size("worker")
    _, steps, q_local, head_width = queries.shape
    _, slots, kv, _ = cache_keys.shape
    rows = steps * q_local
    padded = round_up(rows // kv, 8)
    while kv * padded % 16:
        padded += 8
    full = kv * padded
    query_rows = queries.transpose(0, 2, 1, 3).reshape(rows, head_width)
    dma = pltpu.SemaphoreType.DMA
    bf16, f32 = jnp.bfloat16, jnp.float32
    out = pl.pallas_call(
        functools.partial(kernel, workers, kv, steps),
        out_shape=jax.ShapeDtypeStruct((rows, head_width), bf16),
        in_specs=[pl.BlockSpec(memory_space=pl.ANY)] * 6,
        out_specs=pl.BlockSpec(memory_space=pltpu.VMEM),
        scratch_shapes=[
            pltpu.VMEM((rows, head_width), bf16),
            pltpu.VMEM((full, head_width), f32),
            pltpu.VMEM((full, head_width), bf16),
            pltpu.VMEM((workers, full, head_width), bf16),
            pltpu.VMEM((slots * kv, head_width), bf16),
            pltpu.VMEM((slots * kv, head_width), bf16),
            pltpu.VMEM((steps * kv, head_width), bf16),
            pltpu.VMEM((steps * kv, head_width), bf16),
            pltpu.SMEM(lengths.shape, jnp.int32),
            pltpu.VMEM((padded, slots * kv + lanes), f32),
            pltpu.VMEM((workers, full, head_width), partial_type),
            pltpu.VMEM((workers, full, head_width), partial_type),
            pltpu.VMEM((workers, 2, lanes), f32),
            pltpu.VMEM((workers, 2, lanes), f32),
            dma((6,)),
            dma((workers,)),
            dma((workers,)),
            dma((workers,)),
            dma((workers,)),
            dma((workers,)),
            dma((workers,)),
        ],
        compiler_params=pltpu.CompilerParams(collective_id=0, has_side_effects=True),
    )(
        query_rows,
        cache_keys.reshape(slots * kv, head_width),
        cache_values.reshape(slots * kv, head_width),
        new_keys.reshape(steps * kv, head_width),
        new_values.reshape(steps * kv, head_width),
        lengths,
    )
    return out.reshape(1, q_local, steps, head_width).transpose(0, 2, 1, 3)


def solution(mesh):
    spread = P(("problem", "worker"), None, "head", None)
    return jax.shard_map(
        local,
        mesh=mesh,
        in_specs=(spread,) * 5 + (P(("problem", "worker"), None),),
        out_specs=spread,
        check_vma=False,
    )
```

```python
import functools
import math

import jax
import jax.numpy as jnp
from jax import lax
from jax.experimental import pallas as pl
from jax.experimental.pallas import tpu as pltpu
from jax.sharding import PartitionSpec as P

masked_score = -1e30
lanes = 128
score_chunk = 512
value_chunk = 512
partial_type = jnp.bfloat16


def round_up(number, unit):
    return (number + unit - 1) // unit * unit


def partners_by_distance(own, workers):
    if workers > 8:
        return [lax.rem(own + step, workers) for step in range(1, workers)]
    table = [
        sorted((w for w in range(workers) if w != i), key=lambda w: (abs(w - i), w))
        for i in range(workers)
    ]
    partners = []
    for place in range(workers - 1):
        partner = jnp.int32(table[0][place])
        for i in range(1, workers):
            partner = jnp.where(own == i, table[i][place], partner)
        partners.append(partner)
    return partners


def kernel(
    workers,
    kv,
    steps,
    q_ref,
    k_ref,
    v_ref,
    nk_ref,
    nv_ref,
    len_ref,
    out_ref,
    q_in,
    q_pad,
    q_own,
    q_got,
    keys,
    values,
    new_keys,
    new_values,
    lens,
    score_buf,
    part_send,
    part_got,
    stat_send,
    stat_got,
    load_sem,
    q_send_sem,
    q_recv_sem,
    part_send_sem,
    part_recv_sem,
    stat_send_sem,
    stat_recv_sem,
):
    own = lax.axis_index("worker")
    rows_all, head_width = q_ref.shape
    per = rows_all // kv
    padded = q_pad.shape[0] // kv
    columns = k_ref.shape[0]
    fresh_columns = nk_ref.shape[0]
    factor = head_width ** (-0.5) * math.log2(math.e)
    partners = partners_by_distance(own, workers)

    barrier = pltpu.get_barrier_semaphore()
    for partner in partners:
        pl.semaphore_signal(
            barrier, inc=1, device_id={"worker": partner}, device_id_type=pl.DeviceIdType.MESH
        )

    loads = []
    for place, (source, target) in enumerate(
        (
            (q_ref, q_in),
            (len_ref, lens),
            (nk_ref, new_keys),
            (nv_ref, new_values),
            (k_ref, keys),
            (v_ref, values),
        )
    ):
        loads.append(pltpu.make_async_copy(source, target, load_sem.at[place]))
        loads[-1].start()

    loads[0].wait()
    q_pad[...] = jnp.zeros_like(q_pad)
    q_rows = q_in[...].astype(jnp.float32)
    for head in range(kv):
        q_pad[head * padded : head * padded + per, :] = q_rows[head * per : (head + 1) * per]
    q_own[...] = q_pad[...].astype(jnp.bfloat16)

    pl.semaphore_wait(barrier, workers - 1)
    sends = []

    def send(source, target, send_sem, recv_sem, partner):
        copy = pltpu.make_async_remote_copy(
            src_ref=source,
            dst_ref=target,
            send_sem=send_sem,
            recv_sem=recv_sem,
            device_id={"worker": partner},
            device_id_type=pl.DeviceIdType.MESH,
        )
        copy.start()
        sends.append(copy)

    for place, partner in reversed(list(enumerate(partners))):
        send(q_own, q_got.at[own], q_send_sem.at[place], q_recv_sem.at[own], partner)

    row_id = lax.broadcasted_iota(jnp.int32, (padded, lanes), 0)
    lane_id = lax.broadcasted_iota(jnp.int32, (padded, lanes), 1)
    row_step = lax.rem(row_id, steps)
    lane_head = lax.rem(lane_id, kv)
    loads[1].wait()
    limit = jnp.zeros((padded, lanes), jnp.int32)
    for step in range(steps):
        limit = jnp.where(row_step == step, lens[0, step], limit)
    limit = limit * kv - lane_id

    def fresh_limit(is_own):
        return jnp.minimum((row_step + (1 if is_own else 0)) * kv, fresh_columns) - lane_id

    loads[2].wait()
    loads[3].wait()
    tail = jnp.zeros((lanes - fresh_columns, head_width), jnp.float32)
    fresh_k = jnp.concatenate([new_keys[...].astype(jnp.float32), tail], axis=0)
    fresh_v = jnp.concatenate([new_values[...].astype(jnp.float32), tail], axis=0)
    fresh_k = fresh_k.astype(jnp.bfloat16)
    fresh_v = fresh_v.astype(jnp.bfloat16)

    full_row = lax.broadcasted_iota(jnp.int32, (kv * padded, lanes), 0)
    full_lane = lax.broadcasted_iota(jnp.int32, (kv * padded, lanes), 1)
    diagonal = full_row == full_lane

    def to_row(column):
        return jnp.sum(jnp.where(diagonal, column, 0.0), axis=0, keepdims=True)

    def to_column(row):
        return jnp.sum(jnp.where(diagonal, row, 0.0), axis=1, keepdims=True)

    def attend(queries, count, is_own, value_ready):
        best = [jnp.full((padded, lanes), masked_score, jnp.float32) for _ in range(count)]
        blocks = [
            (start, min(score_chunk, columns - start)) for start in range(0, columns, score_chunk)
        ] + [(columns, lanes)]
        for start, size in blocks:
            block = fresh_k if start == columns else keys[start : start + size, :]
            scores = lax.dot_general(
                queries, block, (((1,), (1,)), ((), ())), preferred_element_type=jnp.float32
            )
            for item in range(count):
                base = item * kv * padded
                for offset in range(0, size, lanes):
                    score = scores[base : base + padded, offset : offset + lanes]
                    for head in range(1, kv):
                        low = base + head * padded
                        score = jnp.where(
                            lane_head == head,
                            scores[low : low + padded, offset : offset + lanes],
                            score,
                        )
                    if start == columns:
                        seen = fresh_limit(is_own) > 0
                    else:
                        seen = limit > start + offset
                    score = jnp.where(seen, score, masked_score)
                    best[item] = jnp.maximum(best[item], score)
                    score_buf[
                        item * padded : (item + 1) * padded,
                        start + offset : start + offset + lanes,
                    ] = score
        maxima, pivots = [], []
        for item in range(count):
            heads = [
                jnp.max(
                    jnp.where(lane_head == head, best[item], masked_score), axis=1, keepdims=True
                )
                for head in range(kv)
            ]
            pivot = jnp.broadcast_to(heads[0], (padded, lanes))
            for head in range(1, kv):
                pivot = jnp.where(lane_head == head, heads[head], pivot)
            maxima.append(to_row(jnp.concatenate(heads, axis=0)))
            pivots.append(pivot)
        sums = [jnp.zeros((padded, lanes), jnp.float32) for _ in range(count)]
        outputs = jnp.zeros((count * kv * padded, head_width), jnp.float32)
        value_ready()
        blocks = [
            (start, min(value_chunk, columns - start)) for start in range(0, columns, value_chunk)
        ] + [(columns, lanes)]
        for start, size in blocks:
            pieces = []
            for offset in range(0, size, lanes):
                stack = []
                for item in range(count):
                    score = score_buf[
                        item * padded : (item + 1) * padded,
                        start + offset : start + offset + lanes,
                    ]
                    weight = jnp.exp2((score - pivots[item]) * factor)
                    sums[item] = sums[item] + weight
                    for head in range(kv):
                        stack.append(jnp.where(lane_head == head, weight, 0.0))
                pieces.append(jnp.concatenate(stack, axis=0).astype(jnp.bfloat16))
            weights = pieces[0] if len(pieces) == 1 else jnp.concatenate(pieces, axis=1)
            block = fresh_v if start == columns else values[start : start + size, :]
            outputs = outputs + jnp.dot(weights, block, preferred_element_type=jnp.float32)
        totals = []
        for item in range(count):
            heads = [
                jnp.sum(jnp.where(lane_head == head, sums[item], 0.0), axis=1, keepdims=True)
                for head in range(kv)
            ]
            totals.append(to_row(jnp.concatenate(heads, axis=0)))
        return maxima, totals, outputs

    loads[4].wait()
    own_max, own_total, own_out = attend(q_own[...], 1, True, loads[5].wait)
    own_max, own_total = own_max[0], own_total[0]

    def answer(place, partner):
        slot = q_got.at[partner]
        pltpu.make_async_copy(slot, slot, q_recv_sem.at[partner]).wait()
        maxima, totals, outputs = attend(q_got[partner], 1, False, lambda: None)
        stat_send[place, 0:1, :] = maxima[0]
        stat_send[place, 1:2, :] = totals[0]
        part_send[place] = outputs.astype(part_send.dtype)
        stat = pltpu.make_async_remote_copy(
            src_ref=stat_send.at[place],
            dst_ref=stat_got.at[own],
            send_sem=stat_send_sem.at[place],
            recv_sem=stat_recv_sem.at[own],
            device_id={"worker": partner},
            device_id_type=pl.DeviceIdType.MESH,
        )
        part = pltpu.make_async_remote_copy(
            src_ref=part_send.at[place],
            dst_ref=part_got.at[own],
            send_sem=part_send_sem.at[place],
            recv_sem=part_recv_sem.at[own],
            device_id={"worker": partner},
            device_id_type=pl.DeviceIdType.MESH,
        )
        stat.start()
        part.start()
        return stat, part

    if workers <= 8:
        for place, partner in enumerate(partners):
            sends.extend(answer(place, partner))
    else:

        def body(place, carry):
            answer(place, lax.rem(own + 1 + place, workers))
            return carry

        lax.fori_loop(0, workers - 1, body, 0)
        for place, partner in enumerate(partners):
            for source, sem in ((stat_send, stat_send_sem), (part_send, part_send_sem)):
                slot = source.at[place]
                pltpu.make_async_copy(slot, slot, sem.at[place]).wait()

    top = own_max
    for partner in partners:
        slot = stat_got.at[partner]
        pltpu.make_async_copy(slot, slot, stat_recv_sem.at[partner]).wait()
        top = jnp.maximum(top, stat_got[partner, 0:1, :])
    own_scale = jnp.exp2((own_max - top) * factor)
    total = own_total * own_scale
    scales = []
    for partner in partners:
        scale = jnp.exp2((stat_got[partner, 0:1, :] - top) * factor)
        total = total + stat_got[partner, 1:2, :] * scale
        scales.append(scale)
    merged = own_out * to_column(own_scale / total)
    columns_of = [to_column(scale / total) for scale in scales]
    for partner, column in zip(partners, columns_of):
        slot = part_got.at[partner]
        pltpu.make_async_copy(slot, slot, part_recv_sem.at[partner]).wait()
        merged = merged + part_got[partner].astype(jnp.float32) * column
    out_ref[...] = jnp.concatenate(
        [merged[head * padded : head * padded + per] for head in range(kv)], axis=0
    ).astype(out_ref.dtype)
    for copy in sends:
        copy.wait_send()


def local(queries, cache_keys, cache_values, new_keys, new_values, lengths):
    workers = lax.axis_size("worker")
    _, steps, q_local, head_width = queries.shape
    _, slots, kv, _ = cache_keys.shape
    rows = steps * q_local
    padded = round_up(rows // kv, 8)
    while kv * padded % 16:
        padded += 8
    full = kv * padded
    query_rows = queries.transpose(0, 2, 1, 3).reshape(rows, head_width)
    dma = pltpu.SemaphoreType.DMA
    bf16, f32 = jnp.bfloat16, jnp.float32
    out = pl.pallas_call(
        functools.partial(kernel, workers, kv, steps),
        out_shape=pltpu.VMEM((rows, head_width), bf16),
        in_specs=[pl.BlockSpec(memory_space=pl.ANY)] * 6,
        out_specs=pl.BlockSpec(memory_space=pltpu.VMEM),
        scratch_shapes=[
            pltpu.VMEM((rows, head_width), bf16),
            pltpu.VMEM((full, head_width), f32),
            pltpu.VMEM((full, head_width), bf16),
            pltpu.VMEM((workers, full, head_width), bf16),
            pltpu.VMEM((slots * kv, head_width), bf16),
            pltpu.VMEM((slots * kv, head_width), bf16),
            pltpu.VMEM((steps * kv, head_width), bf16),
            pltpu.VMEM((steps * kv, head_width), bf16),
            pltpu.SMEM(lengths.shape, jnp.int32),
            pltpu.VMEM((padded, slots * kv + lanes), f32),
            pltpu.VMEM((workers, full, head_width), partial_type),
            pltpu.VMEM((workers, full, head_width), partial_type),
            pltpu.VMEM((workers, 2, lanes), f32),
            pltpu.VMEM((workers, 2, lanes), f32),
            dma((6,)),
            dma((workers,)),
            dma((workers,)),
            dma((workers,)),
            dma((workers,)),
            dma((workers,)),
            dma((workers,)),
        ],
        compiler_params=pltpu.CompilerParams(collective_id=0, has_side_effects=True),
    )(
        query_rows,
        cache_keys.reshape(slots * kv, head_width),
        cache_values.reshape(slots * kv, head_width),
        new_keys.reshape(steps * kv, head_width),
        new_values.reshape(steps * kv, head_width),
        lengths,
    )
    return out.reshape(1, q_local, steps, head_width).transpose(0, 2, 1, 3)


def solution(mesh):
    spread = P(("problem", "worker"), None, "head", None)
    return jax.shard_map(
        local,
        mesh=mesh,
        in_specs=(spread,) * 5 + (P(("problem", "worker"), None),),
        out_specs=spread,
        check_vma=False,
    )
```

```python
import functools
import math

import jax
import jax.numpy as jnp
from jax import lax
from jax.experimental import pallas as pl
from jax.experimental.pallas import tpu as pltpu
from jax.sharding import PartitionSpec as P

masked_score = -1e30
lanes = 128
score_chunk = 512
value_chunk = 512
partial_type = jnp.bfloat16


def round_up(number, unit):
    return (number + unit - 1) // unit * unit


def partners_by_distance(own, workers):
    if workers > 8:
        return [lax.rem(own + step, workers) for step in range(1, workers)]
    table = [
        sorted((w for w in range(workers) if w != i), key=lambda w: (abs(w - i), w))
        for i in range(workers)
    ]
    partners = []
    for place in range(workers - 1):
        partner = jnp.int32(table[0][place])
        for i in range(1, workers):
            partner = jnp.where(own == i, table[i][place], partner)
        partners.append(partner)
    return partners


def kernel(
    workers,
    kv,
    steps,
    q_ref,
    k_ref,
    v_ref,
    nk_ref,
    nv_ref,
    len_ref,
    out_ref,
    q_in,
    q_pad,
    q_own,
    q_got,
    keys,
    values,
    new_keys,
    new_values,
    lens,
    score_buf,
    part_send,
    part_got,
    stat_send,
    stat_got,
    load_sem,
    q_send_sem,
    q_recv_sem,
    part_send_sem,
    part_recv_sem,
    stat_send_sem,
    stat_recv_sem,
):
    own = lax.axis_index("worker")
    rows_all, head_width = q_ref.shape
    per = rows_all // kv
    padded = q_pad.shape[0] // kv
    columns = k_ref.shape[0]
    fresh_columns = nk_ref.shape[0]
    factor = head_width ** (-0.5) * math.log2(math.e)
    partners = partners_by_distance(own, workers)

    barrier = pltpu.get_barrier_semaphore()
    for partner in reversed(partners):
        pl.semaphore_signal(
            barrier, inc=1, device_id={"worker": partner}, device_id_type=pl.DeviceIdType.MESH
        )

    loads = []
    for place, (source, target) in enumerate(
        (
            (q_ref, q_in),
            (len_ref, lens),
            (nk_ref, new_keys),
            (nv_ref, new_values),
            (k_ref, keys),
            (v_ref, values),
        )
    ):
        loads.append(pltpu.make_async_copy(source, target, load_sem.at[place]))
        loads[-1].start()

    loads[0].wait()
    q_pad[...] = jnp.zeros_like(q_pad)
    q_rows = q_in[...].astype(jnp.float32)
    for head in range(kv):
        q_pad[head * padded : head * padded + per, :] = q_rows[head * per : (head + 1) * per]
    q_own[...] = q_pad[...].astype(jnp.bfloat16)

    pl.semaphore_wait(barrier, workers - 1)
    sends = []

    def send(source, target, send_sem, recv_sem, partner):
        copy = pltpu.make_async_remote_copy(
            src_ref=source,
            dst_ref=target,
            send_sem=send_sem,
            recv_sem=recv_sem,
            device_id={"worker": partner},
            device_id_type=pl.DeviceIdType.MESH,
        )
        copy.start()
        sends.append(copy)

    for place, partner in reversed(list(enumerate(partners))):
        send(q_own, q_got.at[own], q_send_sem.at[place], q_recv_sem.at[own], partner)

    row_id = lax.broadcasted_iota(jnp.int32, (padded, lanes), 0)
    lane_id = lax.broadcasted_iota(jnp.int32, (padded, lanes), 1)
    row_step = lax.rem(row_id, steps)
    lane_head = lax.rem(lane_id, kv)
    loads[1].wait()
    limit = jnp.zeros((padded, lanes), jnp.int32)
    for step in range(steps):
        limit = jnp.where(row_step == step, lens[0, step], limit)
    limit = limit * kv - lane_id

    def fresh_limit(is_own):
        return jnp.minimum((row_step + (1 if is_own else 0)) * kv, fresh_columns) - lane_id

    loads[2].wait()
    loads[3].wait()
    tail = jnp.zeros((lanes - fresh_columns, head_width), jnp.float32)
    fresh_k = jnp.concatenate([new_keys[...].astype(jnp.float32), tail], axis=0)
    fresh_v = jnp.concatenate([new_values[...].astype(jnp.float32), tail], axis=0)
    fresh_k = fresh_k.astype(jnp.bfloat16)
    fresh_v = fresh_v.astype(jnp.bfloat16)

    full_row = lax.broadcasted_iota(jnp.int32, (kv * padded, lanes), 0)
    full_lane = lax.broadcasted_iota(jnp.int32, (kv * padded, lanes), 1)
    diagonal = full_row == full_lane

    def to_row(column):
        return jnp.sum(jnp.where(diagonal, column, 0.0), axis=0, keepdims=True)

    def to_column(row):
        return jnp.sum(jnp.where(diagonal, row, 0.0), axis=1, keepdims=True)

    def attend(queries, count, is_own, value_ready):
        best = [jnp.full((padded, lanes), masked_score, jnp.float32) for _ in range(count)]
        blocks = [
            (start, min(score_chunk, columns - start)) for start in range(0, columns, score_chunk)
        ] + [(columns, lanes)]
        for start, size in blocks:
            block = fresh_k if start == columns else keys[start : start + size, :]
            scores = lax.dot_general(
                queries, block, (((1,), (1,)), ((), ())), preferred_element_type=jnp.float32
            )
            for item in range(count):
                base = item * kv * padded
                for offset in range(0, size, lanes):
                    score = scores[base : base + padded, offset : offset + lanes]
                    for head in range(1, kv):
                        low = base + head * padded
                        score = jnp.where(
                            lane_head == head,
                            scores[low : low + padded, offset : offset + lanes],
                            score,
                        )
                    if start == columns:
                        seen = fresh_limit(is_own) > 0
                    else:
                        seen = limit > start + offset
                    score = jnp.where(seen, score, masked_score)
                    best[item] = jnp.maximum(best[item], score)
                    score_buf[
                        item * padded : (item + 1) * padded,
                        start + offset : start + offset + lanes,
                    ] = score
        maxima, pivots = [], []
        for item in range(count):
            heads = [
                jnp.max(
                    jnp.where(lane_head == head, best[item], masked_score), axis=1, keepdims=True
                )
                for head in range(kv)
            ]
            pivot = jnp.broadcast_to(heads[0], (padded, lanes))
            for head in range(1, kv):
                pivot = jnp.where(lane_head == head, heads[head], pivot)
            maxima.append(to_row(jnp.concatenate(heads, axis=0)))
            pivots.append(pivot)
        sums = [jnp.zeros((padded, lanes), jnp.float32) for _ in range(count)]
        outputs = jnp.zeros((count * kv * padded, head_width), jnp.float32)
        value_ready()
        blocks = [
            (start, min(value_chunk, columns - start)) for start in range(0, columns, value_chunk)
        ] + [(columns, lanes)]
        for start, size in blocks:
            pieces = []
            for offset in range(0, size, lanes):
                stack = []
                for item in range(count):
                    score = score_buf[
                        item * padded : (item + 1) * padded,
                        start + offset : start + offset + lanes,
                    ]
                    weight = jnp.exp2((score - pivots[item]) * factor)
                    sums[item] = sums[item] + weight
                    for head in range(kv):
                        stack.append(jnp.where(lane_head == head, weight, 0.0))
                pieces.append(jnp.concatenate(stack, axis=0).astype(jnp.bfloat16))
            weights = pieces[0] if len(pieces) == 1 else jnp.concatenate(pieces, axis=1)
            block = fresh_v if start == columns else values[start : start + size, :]
            outputs = outputs + jnp.dot(weights, block, preferred_element_type=jnp.float32)
        totals = []
        for item in range(count):
            heads = [
                jnp.sum(jnp.where(lane_head == head, sums[item], 0.0), axis=1, keepdims=True)
                for head in range(kv)
            ]
            totals.append(to_row(jnp.concatenate(heads, axis=0)))
        return maxima, totals, outputs

    loads[4].wait()
    own_max, own_total, own_out = attend(q_own[...], 1, True, loads[5].wait)
    own_max, own_total = own_max[0], own_total[0]

    def answer(place, partner):
        slot = q_got.at[partner]
        pltpu.make_async_copy(slot, slot, q_recv_sem.at[partner]).wait()
        maxima, totals, outputs = attend(q_got[partner], 1, False, lambda: None)
        stat_send[place, 0:1, :] = maxima[0]
        stat_send[place, 1:2, :] = totals[0]
        stat = pltpu.make_async_remote_copy(
            src_ref=stat_send.at[place],
            dst_ref=stat_got.at[own],
            send_sem=stat_send_sem.at[place],
            recv_sem=stat_recv_sem.at[own],
            device_id={"worker": partner},
            device_id_type=pl.DeviceIdType.MESH,
        )
        part = pltpu.make_async_remote_copy(
            src_ref=part_send.at[place],
            dst_ref=part_got.at[own],
            send_sem=part_send_sem.at[place],
            recv_sem=part_recv_sem.at[own],
            device_id={"worker": partner},
            device_id_type=pl.DeviceIdType.MESH,
        )
        stat.start()
        part_send[place] = outputs.astype(part_send.dtype)
        part.start()
        return stat, part

    if workers <= 8:
        for place in [0] + list(range(workers - 2, 0, -1)):
            sends.extend(answer(place, partners[place]))
    else:

        def body(place, carry):
            answer(place, lax.rem(own + 1 + place, workers))
            return carry

        lax.fori_loop(0, workers - 1, body, 0)
        for place, partner in enumerate(partners):
            for source, sem in ((stat_send, stat_send_sem), (part_send, part_send_sem)):
                slot = source.at[place]
                pltpu.make_async_copy(slot, slot, sem.at[place]).wait()

    top, total, merged = own_max, own_total, own_out
    for place, partner in enumerate(partners):
        slot = stat_got.at[partner]
        pltpu.make_async_copy(slot, slot, stat_recv_sem.at[partner]).wait()
        part_max, part_total = stat_got[partner, 0:1, :], stat_got[partner, 1:2, :]
        joined = jnp.maximum(top, part_max)
        kept = jnp.exp2((top - joined) * factor)
        added = jnp.exp2((part_max - joined) * factor)
        top, total = joined, total * kept + part_total * added
        if place == workers - 2:
            kept, added = kept / total, added / total
        kept, added = to_column(kept), to_column(added)
        slot = part_got.at[partner]
        pltpu.make_async_copy(slot, slot, part_recv_sem.at[partner]).wait()
        merged = merged * kept + part_got[partner].astype(jnp.float32) * added
    if workers == 1:
        merged = merged * to_column(1.0 / total)
    out_ref[...] = jnp.concatenate(
        [merged[head * padded : head * padded + per] for head in range(kv)], axis=0
    ).astype(out_ref.dtype)
    for copy in sends:
        copy.wait_send()


def local(queries, cache_keys, cache_values, new_keys, new_values, lengths):
    workers = lax.axis_size("worker")
    _, steps, q_local, head_width = queries.shape
    _, slots, kv, _ = cache_keys.shape
    rows = steps * q_local
    padded = round_up(rows // kv, 8)
    while kv * padded % 16:
        padded += 8
    full = kv * padded
    query_rows = queries.transpose(0, 2, 1, 3).reshape(rows, head_width)
    dma = pltpu.SemaphoreType.DMA
    bf16, f32 = jnp.bfloat16, jnp.float32
    out = pl.pallas_call(
        functools.partial(kernel, workers, kv, steps),
        out_shape=pltpu.VMEM((rows, head_width), f32),
        in_specs=[pl.BlockSpec(memory_space=pl.ANY)] * 6,
        out_specs=pl.BlockSpec(memory_space=pltpu.VMEM),
        scratch_shapes=[
            pltpu.VMEM((rows, head_width), bf16),
            pltpu.VMEM((full, head_width), f32),
            pltpu.VMEM((full, head_width), bf16),
            pltpu.VMEM((workers, full, head_width), bf16),
            pltpu.VMEM((slots * kv, head_width), bf16),
            pltpu.VMEM((slots * kv, head_width), bf16),
            pltpu.VMEM((steps * kv, head_width), bf16),
            pltpu.VMEM((steps * kv, head_width), bf16),
            pltpu.SMEM(lengths.shape, jnp.int32),
            pltpu.VMEM((padded, slots * kv + lanes), f32),
            pltpu.VMEM((workers, full, head_width), partial_type),
            pltpu.VMEM((workers, full, head_width), partial_type),
            pltpu.VMEM((workers, 2, lanes), f32),
            pltpu.VMEM((workers, 2, lanes), f32),
            dma((6,)),
            dma((workers,)),
            dma((workers,)),
            dma((workers,)),
            dma((workers,)),
            dma((workers,)),
            dma((workers,)),
        ],
        compiler_params=pltpu.CompilerParams(collective_id=0, has_side_effects=True),
    )(
        query_rows,
        cache_keys.reshape(slots * kv, head_width),
        cache_values.reshape(slots * kv, head_width),
        new_keys.reshape(steps * kv, head_width),
        new_values.reshape(steps * kv, head_width),
        lengths,
    )
    out = out.astype(bf16)
    return out.reshape(1, q_local, steps, head_width).transpose(0, 2, 1, 3)


def solution(mesh):
    spread = P(("problem", "worker"), None, "head", None)
    return jax.shard_map(
        local,
        mesh=mesh,
        in_specs=(spread,) * 5 + (P(("problem", "worker"), None),),
        out_specs=spread,
        check_vma=False,
    )
```

```python
import functools
import math

import jax
import jax.numpy as jnp
from jax import lax
from jax.experimental import pallas as pl
from jax.experimental.pallas import tpu as pltpu
from jax.sharding import PartitionSpec as P

masked_score = -1e30
lanes = 128
score_chunk = 256
value_chunk = 256
partial_type = jnp.bfloat16


def round_up(number, unit):
    return (number + unit - 1) // unit * unit


def partners_by_distance(own, workers):
    if workers > 8:
        return [lax.rem(own + step, workers) for step in range(1, workers)]
    table = [
        sorted((w for w in range(workers) if w != i), key=lambda w: (abs(w - i), w))
        for i in range(workers)
    ]
    partners = []
    for place in range(workers - 1):
        partner = jnp.int32(table[0][place])
        for i in range(1, workers):
            partner = jnp.where(own == i, table[i][place], partner)
        partners.append(partner)
    return partners


def kernel(
    workers,
    kv,
    steps,
    q_ref,
    k_ref,
    v_ref,
    nk_ref,
    nv_ref,
    len_ref,
    out_ref,
    q_in,
    q_pad,
    q_own,
    q_got,
    keys,
    values,
    new_keys,
    new_values,
    lens,
    score_buf,
    part_send,
    part_got,
    stat_send,
    stat_got,
    load_sem,
    q_send_sem,
    q_recv_sem,
    part_send_sem,
    part_recv_sem,
    stat_send_sem,
    stat_recv_sem,
):
    own = lax.axis_index("worker")
    rows_all, head_width = q_ref.shape
    per = rows_all // kv
    padded = q_pad.shape[0] // kv
    columns = k_ref.shape[0]
    fresh_columns = nk_ref.shape[0]
    factor = head_width ** (-0.5) * math.log2(math.e)
    partners = partners_by_distance(own, workers)

    barrier = pltpu.get_barrier_semaphore()
    for partner in reversed(partners):
        pl.semaphore_signal(
            barrier, inc=1, device_id={"worker": partner}, device_id_type=pl.DeviceIdType.MESH
        )

    loads = []
    for place, (source, target) in enumerate(
        (
            (q_ref, q_in),
            (len_ref, lens),
            (nk_ref, new_keys),
            (nv_ref, new_values),
            (k_ref, keys),
            (v_ref, values),
        )
    ):
        loads.append(pltpu.make_async_copy(source, target, load_sem.at[place]))
        loads[-1].start()

    loads[0].wait()
    q_pad[...] = jnp.zeros_like(q_pad)
    q_rows = q_in[...].astype(jnp.float32)
    for head in range(kv):
        q_pad[head * padded : head * padded + per, :] = q_rows[head * per : (head + 1) * per]
    q_own[...] = q_pad[...].astype(jnp.bfloat16)

    pl.semaphore_wait(barrier, workers - 1)
    sends = []

    def send(source, target, send_sem, recv_sem, partner):
        copy = pltpu.make_async_remote_copy(
            src_ref=source,
            dst_ref=target,
            send_sem=send_sem,
            recv_sem=recv_sem,
            device_id={"worker": partner},
            device_id_type=pl.DeviceIdType.MESH,
        )
        copy.start()
        sends.append(copy)

    for place, partner in reversed(list(enumerate(partners))):
        send(q_own, q_got.at[own], q_send_sem.at[place], q_recv_sem.at[own], partner)

    row_id = lax.broadcasted_iota(jnp.int32, (padded, lanes), 0)
    lane_id = lax.broadcasted_iota(jnp.int32, (padded, lanes), 1)
    row_step = lax.rem(row_id, steps)
    lane_head = lax.rem(lane_id, kv)
    loads[1].wait()
    limit = jnp.zeros((padded, lanes), jnp.int32)
    for step in range(steps):
        limit = jnp.where(row_step == step, lens[0, step], limit)
    limit = limit * kv - lane_id

    def fresh_limit(is_own):
        return jnp.minimum((row_step + (1 if is_own else 0)) * kv, fresh_columns) - lane_id

    loads[2].wait()
    loads[3].wait()
    tail = jnp.zeros((lanes - fresh_columns, head_width), jnp.float32)
    fresh_k = jnp.concatenate([new_keys[...].astype(jnp.float32), tail], axis=0)
    fresh_v = jnp.concatenate([new_values[...].astype(jnp.float32), tail], axis=0)
    fresh_k = fresh_k.astype(jnp.bfloat16)
    fresh_v = fresh_v.astype(jnp.bfloat16)

    full_row = lax.broadcasted_iota(jnp.int32, (kv * padded, lanes), 0)
    full_lane = lax.broadcasted_iota(jnp.int32, (kv * padded, lanes), 1)
    diagonal = full_row == full_lane

    def to_row(column):
        return jnp.sum(jnp.where(diagonal, column, 0.0), axis=0, keepdims=True)

    def to_column(row):
        return jnp.sum(jnp.where(diagonal, row, 0.0), axis=1, keepdims=True)

    def attend(queries, count, is_own, value_ready):
        best = [jnp.full((padded, lanes), masked_score, jnp.float32) for _ in range(count)]
        blocks = [
            (start, min(score_chunk, columns - start)) for start in range(0, columns, score_chunk)
        ] + [(columns, lanes)]
        for start, size in blocks:
            block = fresh_k if start == columns else keys[start : start + size, :]
            scores = lax.dot_general(
                queries, block, (((1,), (1,)), ((), ())), preferred_element_type=jnp.float32
            )
            for item in range(count):
                base = item * kv * padded
                for offset in range(0, size, lanes):
                    score = scores[base : base + padded, offset : offset + lanes]
                    for head in range(1, kv):
                        low = base + head * padded
                        score = jnp.where(
                            lane_head == head,
                            scores[low : low + padded, offset : offset + lanes],
                            score,
                        )
                    if start == columns:
                        seen = fresh_limit(is_own) > 0
                    else:
                        seen = limit > start + offset
                    score = jnp.where(seen, score, masked_score)
                    best[item] = jnp.maximum(best[item], score)
                    score_buf[
                        item * padded : (item + 1) * padded,
                        start + offset : start + offset + lanes,
                    ] = score
        maxima, pivots = [], []
        for item in range(count):
            heads = [
                jnp.max(
                    jnp.where(lane_head == head, best[item], masked_score), axis=1, keepdims=True
                )
                for head in range(kv)
            ]
            pivot = jnp.broadcast_to(heads[0], (padded, lanes))
            for head in range(1, kv):
                pivot = jnp.where(lane_head == head, heads[head], pivot)
            maxima.append(to_row(jnp.concatenate(heads, axis=0)))
            pivots.append(pivot)
        sums = [jnp.zeros((padded, lanes), jnp.float32) for _ in range(count)]
        outputs = jnp.zeros((count * kv * padded, head_width), jnp.float32)
        value_ready()
        blocks = [
            (start, min(value_chunk, columns - start)) for start in range(0, columns, value_chunk)
        ] + [(columns, lanes)]
        for start, size in blocks:
            pieces = []
            for offset in range(0, size, lanes):
                stack = []
                for item in range(count):
                    score = score_buf[
                        item * padded : (item + 1) * padded,
                        start + offset : start + offset + lanes,
                    ]
                    weight = jnp.exp2((score - pivots[item]) * factor)
                    sums[item] = sums[item] + weight
                    for head in range(kv):
                        stack.append(jnp.where(lane_head == head, weight, 0.0))
                pieces.append(jnp.concatenate(stack, axis=0).astype(jnp.bfloat16))
            weights = pieces[0] if len(pieces) == 1 else jnp.concatenate(pieces, axis=1)
            block = fresh_v if start == columns else values[start : start + size, :]
            outputs = outputs + jnp.dot(weights, block, preferred_element_type=jnp.float32)
        totals = []
        for item in range(count):
            heads = [
                jnp.sum(jnp.where(lane_head == head, sums[item], 0.0), axis=1, keepdims=True)
                for head in range(kv)
            ]
            totals.append(to_row(jnp.concatenate(heads, axis=0)))
        return maxima, totals, outputs

    loads[4].wait()
    own_max, own_total, own_out = attend(q_own[...], 1, True, loads[5].wait)
    own_max, own_total = own_max[0], own_total[0]

    def answer(place, partner):
        slot = q_got.at[partner]
        pltpu.make_async_copy(slot, slot, q_recv_sem.at[partner]).wait()
        maxima, totals, outputs = attend(q_got[partner], 1, False, lambda: None)
        stat_send[place, 0:1, :] = maxima[0]
        stat_send[place, 1:2, :] = totals[0]
        stat = pltpu.make_async_remote_copy(
            src_ref=stat_send.at[place],
            dst_ref=stat_got.at[own],
            send_sem=stat_send_sem.at[place],
            recv_sem=stat_recv_sem.at[own],
            device_id={"worker": partner},
            device_id_type=pl.DeviceIdType.MESH,
        )
        part = pltpu.make_async_remote_copy(
            src_ref=part_send.at[place],
            dst_ref=part_got.at[own],
            send_sem=part_send_sem.at[place],
            recv_sem=part_recv_sem.at[own],
            device_id={"worker": partner},
            device_id_type=pl.DeviceIdType.MESH,
        )
        stat.start()
        part_send[place] = outputs.astype(part_send.dtype)
        part.start()
        return stat, part

    if workers <= 8:
        for place in [0] + list(range(workers - 2, 0, -1)):
            sends.extend(answer(place, partners[place]))
    else:

        def body(place, carry):
            answer(place, lax.rem(own + 1 + place, workers))
            return carry

        lax.fori_loop(0, workers - 1, body, 0)
        for place, partner in enumerate(partners):
            for source, sem in ((stat_send, stat_send_sem), (part_send, part_send_sem)):
                slot = source.at[place]
                pltpu.make_async_copy(slot, slot, sem.at[place]).wait()

    top, total, merged = own_max, own_total, own_out
    for place, partner in enumerate(partners):
        slot = stat_got.at[partner]
        pltpu.make_async_copy(slot, slot, stat_recv_sem.at[partner]).wait()
        part_max, part_total = stat_got[partner, 0:1, :], stat_got[partner, 1:2, :]
        joined = jnp.maximum(top, part_max)
        kept = jnp.exp2((top - joined) * factor)
        added = jnp.exp2((part_max - joined) * factor)
        top, total = joined, total * kept + part_total * added
        if place == workers - 2:
            kept, added = kept / total, added / total
        kept, added = to_column(kept), to_column(added)
        slot = part_got.at[partner]
        pltpu.make_async_copy(slot, slot, part_recv_sem.at[partner]).wait()
        merged = merged * kept + part_got[partner].astype(jnp.float32) * added
    if workers == 1:
        merged = merged * to_column(1.0 / total)
    out_ref[...] = jnp.concatenate(
        [merged[head * padded : head * padded + per] for head in range(kv)], axis=0
    ).astype(out_ref.dtype)
    for copy in sends:
        copy.wait_send()


def local(queries, cache_keys, cache_values, new_keys, new_values, lengths):
    workers = lax.axis_size("worker")
    _, steps, q_local, head_width = queries.shape
    _, slots, kv, _ = cache_keys.shape
    rows = steps * q_local
    padded = round_up(rows // kv, 8)
    while kv * padded % 16:
        padded += 8
    full = kv * padded
    query_rows = queries.transpose(0, 2, 1, 3).reshape(rows, head_width)
    dma = pltpu.SemaphoreType.DMA
    bf16, f32 = jnp.bfloat16, jnp.float32
    out = pl.pallas_call(
        functools.partial(kernel, workers, kv, steps),
        out_shape=pltpu.VMEM((rows, head_width), f32),
        in_specs=[pl.BlockSpec(memory_space=pl.ANY)] * 6,
        out_specs=pl.BlockSpec(memory_space=pltpu.VMEM),
        scratch_shapes=[
            pltpu.VMEM((rows, head_width), bf16),
            pltpu.VMEM((full, head_width), f32),
            pltpu.VMEM((full, head_width), bf16),
            pltpu.VMEM((workers, full, head_width), bf16),
            pltpu.VMEM((slots * kv, head_width), bf16),
            pltpu.VMEM((slots * kv, head_width), bf16),
            pltpu.VMEM((steps * kv, head_width), bf16),
            pltpu.VMEM((steps * kv, head_width), bf16),
            pltpu.SMEM(lengths.shape, jnp.int32),
            pltpu.VMEM((padded, slots * kv + lanes), f32),
            pltpu.VMEM((workers, full, head_width), partial_type),
            pltpu.VMEM((workers, full, head_width), partial_type),
            pltpu.VMEM((workers, 2, lanes), f32),
            pltpu.VMEM((workers, 2, lanes), f32),
            dma((6,)),
            dma((workers,)),
            dma((workers,)),
            dma((workers,)),
            dma((workers,)),
            dma((workers,)),
            dma((workers,)),
        ],
        compiler_params=pltpu.CompilerParams(collective_id=0, has_side_effects=True),
    )(
        query_rows,
        cache_keys.reshape(slots * kv, head_width),
        cache_values.reshape(slots * kv, head_width),
        new_keys.reshape(steps * kv, head_width),
        new_values.reshape(steps * kv, head_width),
        lengths,
    )
    out = out.astype(bf16)
    return out.reshape(1, q_local, steps, head_width).transpose(0, 2, 1, 3)


def solution(mesh):
    spread = P(("problem", "worker"), None, "head", None)
    return jax.shard_map(
        local,
        mesh=mesh,
        in_specs=(spread,) * 5 + (P(("problem", "worker"), None),),
        out_specs=spread,
        check_vma=False,
    )
```
